512 devices in a mesh: pairs: 128 (over y, z, core), aux: 4 (over x).
Axes of the slice: x: 4, y: 4, z: 16, core: 2. Of those that a mesh axis runs over, the one named last changes fastest.
Arguments:
- fit_left: bfloat16 [2048, 1024, 128], P('pairs', 'aux'), may hold values from -0.1875 to 0.1875
- fit_right: bfloat16 [2048, 1024, 128], P('pairs', 'aux'), may hold values from -6 to 6
- margin: bfloat16 [2048, 16, 128, 128], P(('pairs', 'aux')), may hold values from -1 to 2, as said below
- coupling: float32 [2048, 16], P(('pairs', 'aux')), may hold values from -0.3 to 0.3
- partner: int32 [2048, 16], P(('pairs', 'aux')), may hold values from 0 to 2047, as said below
- virtual: float32 [2048, 128], P(('pairs', 'aux')), may hold values from 0.5 to 4
- occupied: float32 [2048], P(('pairs', 'aux')), may hold values from 0.5 to 2
- counts: int32 [2048], P(('pairs', 'aux')), may hold values from 64 to 128
Outputs:
- amplitude: float32 [2048, 128, 128], P(('pairs', 'aux'))
- residual: float32 [2048, 128, 128], P(('pairs', 'aux'))
The draws below stay inside these ranges and needn't reach their ends.
Inputs may be any that keep to these rules, and one draw needn't show every extreme that they name: A listed pair lies on a device at most 4 places from the listing pair's device along the pairs' order of devices, counted around the end: ((partner[p, k] // 4) - (p // 4)) modulo (512) is at most 4 or at least 508. Each margin block is the identity plus independent entries.
All inputs are finite; a program needn't handle non-finite values.
Results may differ from the reference program's by a relative error of at most 0.012.
The reference program's roundings to bfloat16 on the way (of `rounded`) count: a program that leaves them out, or rounds other values in their place, can miss the bound.
Values may be sent and summed in bfloat16 or wider, within the bound.
No kernel may reach another device: no remote copies, remote signals or barrier semaphores. Data moves between devices by JAX's collectives and lax.ppermute only.
A program may use at most 64 MiB of HBM per device.

```python
import math
import jax
import jax.numpy as jnp
from jax import lax

P_SIZE = 128
NA = 1024
PD = 4
KC = 16
W = 4
ITERS = 2
PAIRS = 2048


def draw_margin(key, part):
    shape = (PAIRS, KC, P_SIZE, P_SIZE)
    noise = jax.random.normal(key, shape, jnp.float32) / P_SIZE ** 0.5
    noise = jnp.clip(noise, -1.0, 1.0)
    return (noise + jnp.eye(P_SIZE, dtype=jnp.float32)).astype(jnp.bfloat16)


def draw_partner(key, part):
    first = jax.random.fold_in(key, 11)
    second = jax.random.fold_in(key, 23)
    device_count = PAIRS // PD
    home = (jnp.arange(PAIRS, dtype=jnp.int32) // PD)[:, None]
    offsets = jax.random.randint(first, (PAIRS, KC), -W, W + 1, dtype=jnp.int32)
    within = jax.random.randint(second, (PAIRS, KC), 0, PD, dtype=jnp.int32)
    return (jnp.mod(home + offsets, device_count) * PD + within).astype(jnp.int32)


def place_ends(result, key, smallest, largest):
    extent = result.shape
    spot = [jax.random.randint(jax.random.fold_in(key, axis), (), 0, extent[axis]) for axis in range(len(extent))]
    result = result.at[tuple(spot)].set(smallest)
    longest = extent.index(max(extent))
    spot[longest] = (spot[longest] + 1) % extent[longest]
    return result.at[tuple(spot)].set(largest)


def shard_levels(own_key, shape, shards, least, top_value):
    def one(axis_at, blocks):
        heights = jax.random.uniform(jax.random.fold_in(jax.random.fold_in(own_key, 6), axis_at), (blocks,), jnp.float32, least / len(shards), top_value / len(shards))
        return jnp.repeat(jnp.exp(heights), shape[axis_at] // blocks).reshape((-1,) + (1,) * (len(shape) - axis_at - 1))

    gain = one(*shards[0])
    for cut in shards[1:]:
        gain = gain * one(*cut)
    return gain


def gaussian(key, shape, scale, reach, cuts=(), kind=jnp.bfloat16):
    entries = scale * jax.random.normal(key, shape, jnp.float32)
    if cuts:
        entries = entries * shard_levels(key, shape, cuts, -0.22, 0.18)
    return jnp.clip(entries, -reach, reach).astype(kind)


def setup_inputs(seed: int = 0) -> dict:
    splits = jax.random.split(jax.random.key(seed), 9)
    fit_left = gaussian(splits[0], (PAIRS, NA, P_SIZE), NA ** -0.5, 0.1875, ((0, 128), (1, 4)))
    fit_right = gaussian(splits[1], (PAIRS, NA, P_SIZE), 1.0, 6.0, ((0, 128), (1, 4)))
    margin = draw_margin(jax.random.fold_in(splits[8], 71), 0)
    coupling = jnp.clip(jax.random.uniform(splits[3], (PAIRS, KC), jnp.float32, -0.3, 0.3) * shard_levels(splits[3], (PAIRS, KC), ((0, 512),), -0.4, 0.0), -0.3, 0.3)
    partner = draw_partner(jax.random.fold_in(splits[8], 71), 0)
    virtual = jnp.clip(jnp.exp(math.log(4.0) - 2.0794415 * jax.random.uniform(splits[5], (PAIRS, P_SIZE), jnp.float32) ** shard_levels(splits[5], (PAIRS, P_SIZE), ((0, 512),), -0.2, 0.2)), 0.5, 4.0)
    occupied = jnp.clip(jnp.exp(math.log(2.0) - 1.3862944 * jax.random.uniform(splits[6], (PAIRS,), jnp.float32) ** shard_levels(splits[6], (PAIRS,), ((0, 512),), -0.2, 0.2)), 0.5, 2.0)
    counts = place_ends(jax.random.randint(splits[7], (PAIRS,), P_SIZE // 2, P_SIZE + 1), jax.random.fold_in(splits[7], 1), P_SIZE // 2, P_SIZE).astype(jnp.int32)
    return {"fit_left": fit_left, "fit_right": fit_right, "margin": margin, "coupling": coupling, "partner": partner, "virtual": virtual, "occupied": occupied, "counts": counts}


def fit_pair(pieces):
    return jnp.dot(pieces[0].T, pieces[1], preferred_element_type=jnp.float32)


def reference(fit_left, fit_right, margin, coupling, partner, virtual, occupied, counts):
    exchange_k = lax.map(fit_pair, (fit_left, fit_right))
    levels = jnp.arange(P_SIZE, dtype=jnp.int32)
    inside = (levels[None, :] < counts[:, None]).astype(jnp.float32)
    valid_cells = inside[:, :, None] * inside[:, None, :]
    exchange_k = exchange_k * valid_cells
    denominator = virtual[:, :, None] + virtual[:, None, :] + occupied[:, None, None]
    amplitude = -exchange_k / denominator
    pair_ids = jnp.arange(PAIRS, dtype=jnp.int32)
    residual = jnp.zeros_like(amplitude)
    for iteration in range(ITERS):
        rounded = amplitude.astype(jnp.bfloat16)

        def visit(carried, index):
            blocks = margin[index].astype(jnp.float32)
            weights = coupling[index]
            targets = partner[index]
            partner_blocks = rounded[targets].astype(jnp.float32)
            left_half = jnp.einsum('kab,kbc->kac', blocks, partner_blocks).astype(jnp.bfloat16)
            left_half = lax.optimization_barrier(left_half).astype(jnp.float32)
            pulled = jnp.einsum('kac,kdc->kad', left_half, blocks)
            pull_sum = jnp.sum(weights[:, None, None] * pulled, axis=0)
            own_block = rounded[index].astype(jnp.float32)
            right_half = jnp.einsum('kba,bc->kac', blocks, own_block).astype(jnp.bfloat16)
            right_half = lax.optimization_barrier(right_half).astype(jnp.float32)
            pushed = jnp.einsum('kac,kcd->kad', right_half, blocks)
            carried = carried.at[targets].add(weights[:, None, None] * pushed)
            return carried, pull_sum

        arrived, pull_sum = lax.scan(visit, jnp.zeros((PAIRS, P_SIZE, P_SIZE), jnp.float32), pair_ids)
        residual = valid_cells * (exchange_k + denominator * amplitude - pull_sum - arrived)
        amplitude = amplitude - residual / denominator
    return amplitude, residual
```

```python
import functools

import jax
import jax.numpy as jnp
from jax import lax
from jax.experimental import pallas as pl
from jax.experimental.pallas import tpu as pltpu
from jax.sharding import PartitionSpec as P

ITERS = 2
PD = 4
KC = 16
N = 128
CL = 16
CHUNK = 4
F32 = jnp.float32
BF16 = jnp.bfloat16
SMEM = pl.BlockSpec(memory_space=pltpu.SMEM)
VMEM = pl.BlockSpec(memory_space=pltpu.VMEM)
HBM = pl.BlockSpec(memory_space=pltpu.HBM)
DMA = pltpu.SemaphoreType.DMA


def shape(dims, dtype):
    return jax.ShapeDtypeStruct(dims, dtype)


def call(body, outs, ins, out_specs, name, scratch=(), limit=20 << 20, flops=1 << 20, moved=1 << 20):
    def place_out(out, spec):
        return pltpu.HBM(out.shape, out.dtype) if spec is HBM else out

    run = pl.pallas_call(
        body,
        out_shape=jax.tree.map(place_out, outs, out_specs),
        in_specs=ins,
        out_specs=out_specs,
        scratch_shapes=scratch,
        compiler_params=pltpu.CompilerParams(vmem_limit_bytes=limit),
        cost_estimate=pl.CostEstimate(flops=flops, bytes_accessed=moved, transcendentals=0),
        name=name,
    )

    def placed(*args):
        return run(
            *[
                pltpu.with_memory_space_constraint(arg, pltpu.HBM) if spec is HBM else arg
                for arg, spec in zip(args, ins)
            ]
        )

    return placed


def dot(a, b):
    return jnp.dot(a, b, preferred_element_type=F32)


def valid_cells(count):
    rows = lax.broadcasted_iota(jnp.int32, (N, N), 0)
    cols = lax.broadcasted_iota(jnp.int32, (N, N), 1)
    return jnp.logical_and(rows < count, cols < count)


def fetch(src, dst, sem, p):
    rows = pl.ds(p * KC, KC)
    return pltpu.make_async_copy(src.at[rows], dst.at[rows], sem.at[p])


def flip_body(s_hbm, out_hbm, s_ref, out_ref, in_sem, out_sem):
    for p in range(PD):
        fetch(s_hbm, s_ref, in_sem, p).start()

    def step(p, _):
        fetch(s_hbm, s_ref, in_sem, p).wait()
        for k in range(KC):
            out_ref[p * KC + k] = s_ref[p * KC + k].T
        fetch(out_ref, out_hbm, out_sem, p).start()
        return 0

    lax.fori_loop(0, PD, step, 0)
    for p in range(PD):
        fetch(out_ref, out_hbm, out_sem, p).wait()


def denominators(virt_ref, occ_ref, p):
    across = jnp.broadcast_to(virt_ref[p : p + 1, :], (N, N))
    return across.T + across + occ_ref[p]


def start_body(occ_ref, cnt_ref, part_ref, virt_ref, k_ref, t_ref, r_ref):
    for p in range(PD):
        total = (part_ref[0, p] + part_ref[1, p]) + (part_ref[2, p] + part_ref[3, p])
        ex = jnp.where(valid_cells(cnt_ref[p]), total, 0.0)
        amp = -ex / denominators(virt_ref, occ_ref, p)
        k_ref[p] = ex
        t_ref[p] = amp
        low = amp.astype(BF16)
        for x in range(4):
            r_ref[x, p] = low


def place(q, here):
    c = q // CL
    group = jnp.where(c == here, 0, jnp.where(c == here + 1 - 2 * (here % 2), 1, 2))
    return group * CL + q % CL


def push_body(
    here_ref, q_ref, w_ref, s_hbm, st_hbm, r_ref, own_ref, h1_hbm, h2_hbm,
    s_ref, st_ref, acc_ref, half_ref, s_sem, st_sem, out_sem,
):
    for p in range(PD):
        fetch(st_hbm, st_ref, st_sem, p).start()
        fetch(s_hbm, s_ref, s_sem, p).start()
    acc_ref[...] = jnp.zeros_like(acc_ref)
    here = here_ref[0]

    def step(p, _):
        fetch(st_hbm, st_ref, st_sem, p).wait()
        fetch(s_hbm, s_ref, s_sem, p).wait()
        low = r_ref[0, p]
        for i in range(0, KC, CHUNK):
            rows = pl.ds(p * KC + i, CHUNK)
            right = dot(st_ref[rows].reshape(CHUNK * N, N), low).astype(BF16)
            for u in range(CHUNK):
                slot = place(q_ref[p, i + u], here)
                acc_ref[slot] += w_ref[p, i + u] * dot(
                    right[u * N : (u + 1) * N], s_ref[p * KC + i + u]
                )
        return 0

    lax.fori_loop(0, PD, step, 0)
    for g, out in enumerate((h1_hbm, h2_hbm)):
        for j in range(CL):
            half_ref[g * CL + j] = acc_ref[(g + 1) * CL + j].astype(BF16)
        pltpu.make_async_copy(half_ref.at[pl.ds(g * CL, CL)], out, out_sem.at[g]).start()
    own_ref[...] = acc_ref[0:CL]
    for g, out in enumerate((h1_hbm, h2_hbm)):
        pltpu.make_async_copy(half_ref.at[pl.ds(g * CL, CL)], out, out_sem.at[g]).wait()


def sum_body(x_ref, own_ref, h1_ref, h2_ref, out_ref, mine_ref):
    x = x_ref[0]
    for j in range(CL):
        out_ref[j] = (own_ref[j] + h1_ref[j].astype(F32) + h2_ref[j].astype(F32)).astype(BF16)
    for p in range(PD):
        j = x * PD + p
        mine_ref[p] = own_ref[j] + h1_ref[j].astype(F32) + h2_ref[j].astype(F32)


def pull_body(
    here_ref, q_ref, w_ref, s_hbm, st_hbm, t0_hbm, t1_hbm, t2_hbm, out_ref,
    s_ref, st_ref, win_ref, s_sem, st_sem, t_sem,
):
    def window(g):
        src = (t0_hbm, t1_hbm, t2_hbm)[g]
        return pltpu.make_async_copy(src, win_ref.at[pl.ds(g * CL, CL)], t_sem.at[g])

    for g in range(3):
        window(g).start()
    for p in range(PD):
        fetch(s_hbm, s_ref, s_sem, p).start()
        fetch(st_hbm, st_ref, st_sem, p).start()
    for g in range(3):
        window(g).wait()
    here = here_ref[0]

    def step(p, _):
        fetch(s_hbm, s_ref, s_sem, p).wait()
        fetch(st_hbm, st_ref, st_sem, p).wait()
        left = [
            dot(s_ref[p * KC + k], win_ref[place(q_ref[p, k], here)]).astype(BF16)
            for k in range(KC)
        ]
        total = jnp.zeros((N, N), F32)
        for k in range(KC):
            total = total + w_ref[p, k] * dot(left[k], st_ref[p * KC + k])
        out_ref[p] = total
        return 0

    lax.fori_loop(0, PD, step, 0)


def update_body(
    last, x_ref, occ_ref, cnt_ref, virt_ref, k_ref, t_ref, pull_ref, got_ref, mine_ref, t_out, r_out
):
    x = x_ref[0]
    for p in range(PD):
        arrived = mine_ref[p]
        for s in range(4):
            arrived = arrived + jnp.where(x == s, 0.0, got_ref[s, p].astype(F32))
        den = denominators(virt_ref, occ_ref, p)
        res = k_ref[p] + den * t_ref[p] - pull_ref[p] - arrived
        res = jnp.where(valid_cells(cnt_ref[p]), res, 0.0)
        amp = t_ref[p] - res / den
        t_out[p] = amp
        if last:
            r_out[p] = res
        else:
            low = amp.astype(BF16)
            for s in range(4):
                r_out[s, p] = low


def swap_chip(value):
    count = lax.axis_size("pairs")
    return lax.ppermute(value, "pairs", [(i, i ^ 1) for i in range(count)])


def swap_next(value):
    count = lax.axis_size("pairs")
    return lax.ppermute(
        value, "pairs", [(i, (i + 2 * (i % 2) - 1) % count) for i in range(count)]
    )


def across(value):
    return lax.all_to_all(value, "aux", 0, 0, tiled=True)


def shards(fit_left, fit_right, margin, coupling, partner, virtual, occupied, counts):
    here = lax.axis_index("pairs").reshape(1)
    x = lax.axis_index("aux").reshape(1)
    blocks = margin.reshape(PD * KC, N, N)
    square = shape((PD, N, N), F32)
    cluster = shape((CL, N, N), BF16)
    wide = shape((4, PD, N, N), BF16)
    link_flops = PD * KC * 4 * N**3

    fitted = jnp.einsum("nqa,nqb->nab", fit_left, fit_right, preferred_element_type=F32)
    partial = across(fitted.reshape(4, PD, N, N))
    links = (PD * KC, N, N)
    every = [pltpu.VMEM(links, BF16), pltpu.VMEM(links, BF16)]
    flipped = call(
        flip_body,
        shape(links, BF16),
        [HBM],
        HBM,
        "flip",
        scratch=every + [DMA((PD,)), DMA((PD,))],
        moved=4 << 20,
    )(blocks)
    exchange, amp, low = call(
        start_body,
        (square, square, wide),
        [SMEM, SMEM, VMEM, VMEM],
        (VMEM, VMEM, VMEM),
        "start",
        moved=2 << 20,
    )(occupied, counts, partial, virtual)
    for it in range(ITERS):
        last = it == ITERS - 1
        own_t = across(low).reshape(CL, N, N)
        own, h1, h2 = call(
            push_body,
            (shape((CL, N, N), F32), cluster, cluster),
            [SMEM, SMEM, SMEM, HBM, HBM, VMEM],
            (VMEM, HBM, HBM),
            "push",
            scratch=every
            + [
                pltpu.VMEM((3 * CL, N, N), F32),
                pltpu.VMEM((2 * CL, N, N), BF16),
                DMA((PD,)),
                DMA((PD,)),
                DMA((2,)),
            ],
            flops=link_flops,
            moved=6 << 20,
        )(here, partner, coupling, blocks, flipped, low)
        g1 = swap_chip(h1)
        g2 = swap_next(h2)
        t1 = swap_chip(own_t)
        t2 = swap_next(own_t)
        sums, mine = call(
            sum_body, (cluster, square), [SMEM, VMEM, VMEM, VMEM], (VMEM, VMEM), "sum", moved=3 << 20
        )(x, own, g1, g2)
        got = across(sums.reshape(4, PD, N, N))
        pulled = call(
            pull_body,
            square,
            [SMEM, SMEM, SMEM, HBM, HBM, HBM, HBM, HBM],
            VMEM,
            "pull",
            scratch=every + [pltpu.VMEM((3 * CL, N, N), BF16), DMA((PD,)), DMA((PD,)), DMA((3,))],
            flops=link_flops,
            moved=6 << 20,
        )(here, partner, coupling, blocks, flipped, own_t, t1, t2)
        amp, low = call(
            functools.partial(update_body, last),
            (square, square if last else wide),
            [SMEM, SMEM, SMEM] + [VMEM] * 6,
            (VMEM, VMEM),
            "update",
            moved=3 << 20,
        )(x, occupied, counts, virtual, exchange, amp, pulled, got, mine)
    return (amp, low)


def solution(mesh):
    both = ("pairs", "aux")
    in_specs = (
        P("pairs", "aux", None),
        P("pairs", "aux", None),
        P(both, None, None, None),
        P(both, None),
        P(both, None),
        P(both, None),
        P(both),
        P(both),
    )
    out_specs = (P(both, None, None), P(both, None, None))
    return jax.shard_map(shards, mesh=mesh, in_specs=in_specs, out_specs=out_specs, check_vma=False)
```

```python
import functools

import jax
import jax.numpy as jnp
from jax import lax
from jax.experimental import pallas as pl
from jax.experimental.pallas import tpu as pltpu
from jax.sharding import PartitionSpec as P


ITERS = 2
PD = 4
KC = 16
N = 128
CL = 16
CHUNK = 4
STEP = 32
F32 = jnp.float32
BF16 = jnp.bfloat16
SMEM = pl.BlockSpec(memory_space=pltpu.SMEM)
VMEM = pl.BlockSpec(memory_space=pltpu.VMEM)
HBM = pl.BlockSpec(memory_space=pltpu.HBM)
ANY = pl.BlockSpec(memory_space=pl.ANY)
DMA = pltpu.SemaphoreType.DMA


def shape(dims, dtype):
    return jax.ShapeDtypeStruct(dims, dtype)


def call(body, outs, ins, out_specs, scratch=(), limit=20 << 20, flops=1 << 20, moved=1 << 20):
    def place_out(out, spec):
        return pltpu.HBM(out.shape, out.dtype) if spec is HBM else out

    run = pl.pallas_call(
        body,
        out_shape=jax.tree.map(place_out, outs, out_specs),
        in_specs=ins,
        out_specs=out_specs,
        scratch_shapes=scratch,
        compiler_params=pltpu.CompilerParams(vmem_limit_bytes=limit),
        cost_estimate=pl.CostEstimate(flops=flops, bytes_accessed=moved, transcendentals=0),
    )

    def placed(*args):
        return run(
            *[
                pltpu.with_memory_space_constraint(arg, pltpu.HBM) if spec is HBM else arg
                for arg, spec in zip(args, ins)
            ]
        )

    return placed


def dot(a, b):
    return jnp.dot(a, b, preferred_element_type=F32)


def valid_cells(count):
    rows = lax.broadcasted_iota(jnp.int32, (N, N), 0)
    cols = lax.broadcasted_iota(jnp.int32, (N, N), 1)
    return jnp.logical_and(rows < count, cols < count)


def part(src, dst, sem, i, rows=KC):
    place = pl.ds(i * rows, rows)
    return pltpu.make_async_copy(src.at[place], dst.at[place], sem.at[i])


def fit_body(l_hbm, r_hbm, out_hbm, l_ref, r_ref, out_ref, l_sem, r_sem, out_sem):
    for i in range(4):
        part(l_hbm, l_ref, l_sem, i, PD).start()
        part(r_hbm, r_ref, r_sem, i, PD).start()
    for i in range(4):
        part(l_hbm, l_ref, l_sem, i, PD).wait()
        part(r_hbm, r_ref, r_sem, i, PD).wait()
        for j in range(i * PD, i * PD + PD):
            out_ref[j] = lax.dot_general(
                l_ref[j], r_ref[j], (((0,), (0,)), ((), ())), preferred_element_type=F32
            )
        part(out_ref, out_hbm, out_sem, i, PD).start()
    for i in range(4):
        part(out_ref, out_hbm, out_sem, i, PD).wait()


def flip_body(s_hbm, out_hbm, s_ref, out_ref, in_sem, out_sem):
    for p in range(PD):
        part(s_hbm, s_ref, in_sem, p).start()

    def step(p, _):
        part(s_hbm, s_ref, in_sem, p).wait()
        for k in range(KC):
            out_ref[p * KC + k] = s_ref[p * KC + k].T
        part(out_ref, out_hbm, out_sem, p).start()
        return 0

    lax.fori_loop(0, PD, step, 0)
    for p in range(PD):
        part(out_ref, out_hbm, out_sem, p).wait()


def denominators(virt_ref, occ_ref, p):
    across = jnp.broadcast_to(virt_ref[p : p + 1, :], (N, N))
    return across.T + across + occ_ref[p]


def spread(low_ref, out_hbm, sem):
    return [pltpu.make_async_copy(low_ref, out_hbm.at[x], sem.at[x]) for x in range(4)]


def start_body(
    occ_ref, cnt_ref, part_ref, virt_ref, k_hbm, t_hbm, r_hbm, low_ref, k_ref, t_ref, sem, low_sem
):
    for p in range(PD):
        total = (part_ref[0, p] + part_ref[1, p]) + (part_ref[2, p] + part_ref[3, p])
        ex = jnp.where(valid_cells(cnt_ref[p]), total, 0.0)
        amp = -ex / denominators(virt_ref, occ_ref, p)
        k_ref[p] = ex
        t_ref[p] = amp
        low_ref[p] = amp.astype(BF16)
    copies = spread(low_ref, r_hbm, low_sem)
    copies += [
        pltpu.make_async_copy(k_ref, k_hbm, sem.at[0]),
        pltpu.make_async_copy(t_ref, t_hbm, sem.at[1]),
    ]
    for copy in copies:
        copy.start()
    for copy in copies:
        copy.wait()


def place(q, here):
    c = q // CL
    group = jnp.where(c == here, 0, jnp.where(c == here + 1 - 2 * (here % 2), 1, 2))
    return group * CL + q % CL


def push_body(
    here_ref, q_ref, w_ref, s_hbm, st_hbm, r_ref, own_ref, h1_ref, h2_ref,
    s_ref, st_ref, acc_ref, s_sem, st_sem,
):
    def load(i):
        part(st_hbm, st_ref, st_sem, i, STEP).start()
        part(s_hbm, s_ref, s_sem, i, STEP).start()

    for j in range(PD * KC // STEP):
        load(j)
    acc_ref[...] = jnp.zeros_like(acc_ref)
    here = here_ref[0]
    for i in range(0, PD * KC, CHUNK):
        if i % STEP == 0:
            part(st_hbm, st_ref, st_sem, i // STEP, STEP).wait()
            part(s_hbm, s_ref, s_sem, i // STEP, STEP).wait()
        p, k = divmod(i, KC)
        right = dot(st_ref[i : i + CHUNK].reshape(CHUNK * N, N), r_ref[p]).astype(BF16)
        for u in range(CHUNK):
            slot = place(q_ref[p, k + u], here)
            acc_ref[slot] += w_ref[p, k + u] * dot(right[u * N : (u + 1) * N], s_ref[i + u])
    for j in range(CL):
        h2_ref[j] = acc_ref[2 * CL + j].astype(BF16)
        h1_ref[j] = acc_ref[CL + j].astype(BF16)
    own_ref[...] = acc_ref[0:CL]


def sum_body(own_ref, h1_ref, h2_ref, out_hbm, out_ref, sem):
    for i in range(4):
        for j in range(i * PD, i * PD + PD):
            out_ref[j] = (own_ref[j] + h1_ref[j].astype(F32) + h2_ref[j].astype(F32)).astype(BF16)
        part(out_ref, out_hbm, sem, i, PD).start()
    for i in range(4):
        part(out_ref, out_hbm, sem, i, PD).wait()


def pull_body(
    here_ref, q_ref, w_ref, s_hbm, st_hbm, t0_hbm, t1_hbm, t2_hbm, out_ref,
    s_ref, st_ref, win_ref, s_sem, st_sem, t_sem,
):
    windows = [
        pltpu.make_async_copy(src, win_ref.at[pl.ds(g * CL, CL)], t_sem.at[g])
        for g, src in enumerate((t0_hbm, t1_hbm, t2_hbm))
    ]

    def load(i):
        part(s_hbm, s_ref, s_sem, i, STEP).start()
        part(st_hbm, st_ref, st_sem, i, STEP).start()

    for copy in windows:
        copy.start()
    for j in range(PD * KC // STEP):
        load(j)
    for copy in windows:
        copy.wait()
    here = here_ref[0]
    for p in range(PD):
        left = []
        for k in range(KC):
            if (p * KC + k) % STEP == 0:
                part(s_hbm, s_ref, s_sem, (p * KC + k) // STEP, STEP).wait()
            left.append(
                dot(s_ref[p * KC + k], win_ref[place(q_ref[p, k], here)]).astype(BF16)
            )
        total = jnp.zeros((N, N), F32)
        for k in range(KC):
            if (p * KC + k) % STEP == 0:
                part(st_hbm, st_ref, st_sem, (p * KC + k) // STEP, STEP).wait()
            total = total + w_ref[p, k] * dot(left[k], st_ref[p * KC + k])
        out_ref[p] = total


def update_body(
    last, occ_ref, cnt_ref, virt_ref, k_ref, t_ref, pull_ref, got_ref, t_hbm, r_hbm,
    *rest,
):
    low_ref, new_ref, sem, low_sem = rest
    copies = []
    for p in range(PD):
        arrived = (got_ref[0, p].astype(F32) + got_ref[1, p].astype(F32)) + (
            got_ref[2, p].astype(F32) + got_ref[3, p].astype(F32)
        )
        den = denominators(virt_ref, occ_ref, p)
        res = k_ref[p] + den * t_ref[p] - pull_ref[p] - arrived
        res = jnp.where(valid_cells(cnt_ref[p]), res, 0.0)
        amp = t_ref[p] - res / den
        new_ref[p] = amp
        low_ref[p] = res if last else amp.astype(BF16)
        if last:
            copies.append(pltpu.make_async_copy(low_ref.at[p], r_hbm.at[p], low_sem.at[p]))
            copies[-1].start()
        copies.append(pltpu.make_async_copy(new_ref.at[p], t_hbm.at[p], sem.at[p]))
        copies[-1].start()
    if not last:
        more = spread(low_ref, r_hbm, low_sem)
        for copy in more:
            copy.start()
        copies += more
    for copy in copies:
        copy.wait()


def swap_chip(value):
    count = lax.axis_size("pairs")
    return lax.ppermute(value, "pairs", [(i, i ^ 1) for i in range(count)])


def swap_next(value):
    count = lax.axis_size("pairs")
    return lax.ppermute(
        value, "pairs", [(i, (i + 2 * (i % 2) - 1) % count) for i in range(count)]
    )


def across(value):
    return lax.all_to_all(value, "aux", 0, 0, tiled=True)


def shards(fit_left, fit_right, margin, coupling, partner, virtual, occupied, counts):
    here = lax.axis_index("pairs").reshape(1)
    blocks = margin.reshape(PD * KC, N, N)
    square = shape((PD, N, N), F32)
    cluster = shape((CL, N, N), BF16)
    wide = shape((4, PD, N, N), BF16)
    link_flops = PD * KC * 4 * N**3

    high_block = pltpu.VMEM((PD, N, N), F32)
    fitted = call(
        fit_body,
        shape((CL, N, N), F32),
        [HBM, HBM],
        HBM,
        scratch=[pltpu.VMEM(fit_left.shape, BF16)] * 2 + [pltpu.VMEM((CL, N, N), F32)] + [DMA((4,))] * 3,
        moved=5 << 20,
    )(fit_left, fit_right)
    partial = across(fitted.reshape(4, PD, N, N))
    links = (PD * KC, N, N)
    every = [pltpu.VMEM(links, BF16), pltpu.VMEM(links, BF16)]
    flipped = call(
        flip_body,
        shape(links, BF16),
        [HBM],
        HBM,
        scratch=every + [DMA((PD,)), DMA((PD,))],
        moved=4 << 20,
    )(blocks)
    exchange, amp, low, mine = call(
        start_body,
        (square, square, wide, shape((PD, N, N), BF16)),
        [SMEM, SMEM, VMEM, VMEM],
        (HBM, HBM, HBM, VMEM),
        scratch=[high_block, high_block, DMA((2,)), DMA((4,))],
        moved=2 << 20,
    )(occupied, counts, partial, virtual)
    for it in range(ITERS):
        last = it == ITERS - 1
        own_t = across(low).reshape(CL, N, N)
        own, h1, h2 = call(
            push_body,
            (shape((CL, N, N), F32), cluster, cluster),
            [SMEM, SMEM, SMEM, HBM, HBM, VMEM],
            (VMEM, VMEM, VMEM),
            scratch=every
            + [pltpu.VMEM((3 * CL, N, N), F32), DMA((PD * KC // STEP,)), DMA((PD * KC // STEP,))],
            flops=link_flops,
            moved=6 << 20,
        )(here, partner, coupling, blocks, flipped, mine)
        g2 = swap_next(h2)
        g1 = swap_chip(h1)
        t2 = swap_next(own_t)
        t1 = swap_chip(own_t)
        sums = call(
            sum_body,
            cluster,
            [VMEM, VMEM, VMEM],
            HBM,
            scratch=[pltpu.VMEM((CL, N, N), BF16), DMA((4,))],
            moved=3 << 20,
        )(own, g1, g2)
        got = across(sums.reshape(4, PD, N, N))
        pulled = call(
            pull_body,
            square,
            [SMEM, SMEM, SMEM, HBM, HBM, ANY, ANY, ANY],
            VMEM,
            scratch=every
            + [pltpu.VMEM((3 * CL, N, N), BF16), DMA((PD * KC // STEP,)), DMA((PD * KC // STEP,)), DMA((3,))],
            flops=link_flops,
            moved=6 << 20,
        )(here, partner, coupling, blocks, flipped, own_t, t1, t2)
        outs = (square, square) if last else (square, wide, shape((PD, N, N), BF16))
        amp, low, *more = call(
            functools.partial(update_body, last),
            outs,
            [SMEM, SMEM] + [VMEM] * 5,
            (HBM, HBM) if last else (HBM, HBM, VMEM),
            scratch=([high_block] if last else []) + [high_block, DMA((PD,)), DMA((PD,))],
            moved=3 << 20,
        )(occupied, counts, virtual, exchange, amp, pulled, got)
        mine = more[0] if more else None
    return (amp, low)


def solution(mesh):
    both = ("pairs", "aux")
    in_specs = (
        P("pairs", "aux", None),
        P("pairs", "aux", None),
        P(both, None, None, None),
        P(both, None),
        P(both, None),
        P(both, None),
        P(both),
        P(both),
    )
    out_specs = (P(both, None, None), P(both, None, None))

    return jax.shard_map(shards, mesh=mesh, in_specs=in_specs, out_specs=out_specs, check_vma=False)
```
